32 devices in a mesh: group: 2 (over x), blk: 16 (over z, y, core).
Axes of the slice: x: 2, y: 2, z: 4, core: 2. Of those that a mesh axis runs over, the one named last changes fastest.
Arguments:
- spectra: bfloat16 [2, 2048, 768], P(None, ('group', 'blk')), parts along dimension 1, may hold values from -6 to 6
- gap_mask: int32 [2048, 48], P(('group', 'blk')), parts along dimension 0, may hold values 0 or 1
Outputs:
- correlation: float32 [8, 2048, 1024], P(None, ('group', 'blk')), parts along dimension 1
The draws below stay inside these ranges and needn't reach their ends.
There are 2 independent parts, one for each index of `group`. The reference program is written for one: setup_inputs(seed, part) draws one part's arguments, and reference() takes and returns one part's arrays. A program takes and returns all parts, laid end to end along the dimension named above; each array names one. Nothing has to cross between parts.
All inputs are finite; a program needn't handle non-finite values. No bound on the sum of `gap_mask` on one device may be relied on, other than what follows from the above.
Results may differ from the reference program's by a relative error of at most 0.0085.
Values may be sent and summed in bfloat16 or wider, within the bound.
A program may use at most 192 MiB of HBM per device.

```python
import math
import jax
import jax.numpy as jnp
from jax import lax

STA_DEV = 64
WINDOWS = 48
BINS = 16
LAGS = 8
STATIONS = 1024
N_BLK = 16


def touch_ends(values, rng, smallest, largest):
    longest = values.shape.index(max(values.shape))
    spots = []
    for shift in (0, 1):
        where = [jax.random.randint(jax.random.fold_in(rng, axis), (), 0, length) for axis, length in enumerate(values.shape)]
        where[longest] = (where[longest] + shift) % values.shape[longest]
        spots.append(tuple(where))
    return values.at[spots[0]].set(smallest).at[spots[1]].set(largest)


def block_scale(rng, shape, split, smallest, largest):
    def one(axis_at, blocks):
        heights = jax.random.uniform(jax.random.fold_in(jax.random.fold_in(rng, 6), axis_at), (blocks,), jnp.float32, smallest / len(split), largest / len(split))
        return jnp.repeat(jnp.exp(heights), shape[axis_at] // blocks).reshape((-1,) + (1,) * (len(shape) - axis_at - 1))

    level = one(*split[0])
    for cut in split[1:]:
        level = level * one(*cut)
    return level


def bell_draw(rng, dims, deviation, most, pieces=(), held_as=jnp.bfloat16):
    entries = deviation * jax.random.normal(rng, dims, jnp.float32)
    if pieces:
        entries = entries * block_scale(rng, dims, pieces, -0.22, 0.18)
    return jnp.clip(entries, -most, most).astype(held_as)


def setup_inputs(seed: int = 0, part: int = 0) -> dict:
    splits = jax.random.split(jax.random.key(seed), 3)
    part_splits = jax.random.split(jax.random.fold_in(splits[2], part), 3)
    return {
        "spectra": bell_draw(part_splits[0], (2, STATIONS, WINDOWS * BINS), 1.0, 6.0, ((1, 16),)),
        "gap_mask": touch_ends((jax.random.randint(part_splits[1], (STATIONS, WINDOWS), 0, 8) < 7).astype(jnp.int32), jax.random.fold_in(part_splits[1], 1), 0, 1),
    }


level_floor = 0.3
first_bin = 96.0

def band_table(bin_count):
    ladder = jnp.arange(bin_count, dtype=jnp.int32)
    near = (jnp.abs(ladder[:, None] - ladder[None, :]) <= 2).astype(jnp.float32)
    return near / lax.optimization_barrier(jnp.sum(near, axis=0, keepdims=True))

def phase_tables(bin_count, lag_count):
    freq = first_bin + jnp.arange(bin_count, dtype=jnp.float32)
    shifts = 3.0 + 5.0 * jnp.arange(lag_count, dtype=jnp.float32)
    theta = 2.0 * math.pi * freq[:, None] * shifts[None, :] / 512.0
    return (jnp.cos(theta), jnp.sin(theta))

def whiten(spectra, gap_mask):
    members = spectra.shape[1]
    win_count = gap_mask.shape[1]
    bin_count = spectra.shape[2] // win_count
    parts = spectra.astype(jnp.float32).reshape(2, members, win_count, bin_count)
    amplitude = jnp.sqrt(parts[0] * parts[0] + parts[1] * parts[1])
    level = jnp.einsum('swg,gf->swf', amplitude, band_table(bin_count), precision=lax.Precision.HIGHEST)
    level = jnp.maximum(level, level_floor)
    factor = gap_mask.astype(jnp.float32)[None, :, :, None] / level[None]
    return (parts * factor).astype(jnp.bfloat16)

def modulate(whitened, lag_count):
    win_count = whitened.shape[2]
    bin_count = whitened.shape[3]
    cosine, sine = phase_tables(bin_count, lag_count)
    scale = 1.0 / math.sqrt(win_count * bin_count)
    values = whitened.astype(jnp.float32)
    cos_rows = cosine.T[:, None, None, None, :]
    sin_rows = sine.T[:, None, None, None, :]
    even_mod = (cos_rows * values[None] * scale).astype(jnp.bfloat16)
    swapped = jnp.stack([values[1], -values[0]])
    odd_mod = (sin_rows * swapped[None] * scale).astype(jnp.bfloat16)
    return jnp.stack([even_mod, odd_mod])

def reference(spectra, gap_mask):
    whitened = whiten(spectra, gap_mask)
    modulated = modulate(whitened, LAGS)
    flat_white = whitened.astype(jnp.float32).reshape(2, STATIONS, WINDOWS * BINS)

    def one_block(block_id):
        start = (block_id * STA_DEV).astype(jnp.int32)
        piece = lax.dynamic_slice_in_dim(modulated, start, STA_DEV, 3)
        piece = piece.astype(jnp.float32).reshape(2, LAGS, 2, STA_DEV, WINDOWS * BINS)
        terms = jnp.einsum('hjcsk,ctk->hjst', piece, flat_white, precision=lax.Precision.HIGHEST)
        return terms[0] - terms[1]
    blocks = lax.map(one_block, jnp.arange(N_BLK, dtype=jnp.int32))
    return jnp.transpose(blocks, (1, 0, 2, 3)).reshape(LAGS, STATIONS, STATIONS)
```

```python
import functools
import math

import jax
import jax.numpy as jnp
import numpy as np
from jax import lax
from jax.experimental import pallas as pl
from jax.experimental.pallas import tpu as pltpu
from jax.sharding import PartitionSpec as P

LAGS = 8
LANES = 128
level_floor = 0.3
first_bin = 96.0
reach = 2


def phase_tables(bin_count, lag_count, scale):
    freq = first_bin + np.arange(bin_count, dtype=np.float32)
    shifts = 3.0 + 5.0 * np.arange(lag_count, dtype=np.float32)
    theta = np.float32(2.0 * math.pi) * freq[None, :] * shifts[:, None] / np.float32(512.0)
    tables = np.stack([np.cos(theta), np.sin(theta)]) * np.float32(scale)
    return np.tile(tables, (1, 1, LANES // bin_count)).astype(np.float32)


def kernel(
    devices, spectra, gaps, tables, out, blocks, modulated,
    ring_send, ring_recv, pair_send, pair_recv,
):
    members, length = spectra.shape[1], spectra.shape[2]
    windows = gaps.shape[0]
    bins = length // windows
    lag_count = out.shape[0]
    half = members // 2
    chips = devices // 2
    far = chips // 2
    turn = (chips + 1) // 2

    me = lax.axis_index("blk")
    chip, core = me // 2, me % 2
    spot = jnp.where(chip % 2 == 0, chip // 2, chips - 1 - chip // 2)

    def chip_at(position):
        position = (position + 2 * chips) % chips
        return jnp.where(position < turn, 2 * position, 2 * chips - 1 - 2 * position)

    targets = (chip_at(spot + 1) * 2 + core, chip_at(spot - 1) * 2 + core)
    partner = chip * 2 + (1 - core)

    def source_chip(way, distance):
        return chip_at(spot - distance if way == 0 else spot + distance)

    def piece(block, h):
        return blocks.at[block, pl.ds(h * half, half), :]

    def ring(way, step, h, incoming=False):
        place = piece(source_chip(way, step + 1 if incoming else step) * 2 + core, h)
        return pltpu.make_async_remote_copy(
            src_ref=place, dst_ref=place,
            send_sem=ring_send.at[way, step, h], recv_sem=ring_recv.at[way, step, h],
            device_id={"blk": targets[way]}, device_id_type=pl.DeviceIdType.MESH,
        )

    def pair(way, distance, h, incoming=False):
        side = 1 - core if incoming else core
        place = piece(source_chip(way, distance) * 2 + side, h)
        return pltpu.make_async_remote_copy(
            src_ref=place, dst_ref=place,
            send_sem=pair_send.at[way, distance, h], recv_sem=pair_recv.at[way, distance, h],
            device_id={"blk": partner}, device_id_type=pl.DeviceIdType.MESH,
        )

    barrier = pltpu.get_barrier_semaphore()
    for other in (*targets, partner):
        pl.semaphore_signal(
            barrier, inc=1, device_id={"blk": other}, device_id_type=pl.DeviceIdType.MESH
        )

    window_of = lax.broadcasted_iota(jnp.int32, (windows, length), 1) // bins
    spread = window_of == lax.broadcasted_iota(jnp.int32, (windows, length), 0)
    live = lax.dot_general(
        gaps[...].astype(jnp.float32).astype(jnp.bfloat16),
        spread.astype(jnp.float32).astype(jnp.bfloat16),
        (((0,), (0,)), ((), ())),
        preferred_element_type=jnp.float32,
    )
    bin_of = lax.broadcasted_iota(jnp.int32, (members, LANES), 1) % bins
    count = 1 + jnp.minimum(bin_of, reach) + jnp.minimum(bins - 1 - bin_of, reach)
    weight = 1.0 / count.astype(jnp.float32)
    for at in range(0, length, LANES):
        cut = slice(at, at + LANES)
        real = spectra[0, :, cut].astype(jnp.float32)
        imag = spectra[1, :, cut].astype(jnp.float32)
        amplitude = jnp.sqrt(real * real + imag * imag)
        total = amplitude
        for off in range(1, reach + 1):
            total += jnp.where(bin_of >= off, pltpu.roll(amplitude, off, 1), 0.0)
            total += jnp.where(bin_of < bins - off, pltpu.roll(amplitude, LANES - off, 1), 0.0)
        level = jnp.maximum(total * weight, level_floor)
        factor = live[:, cut] / level
        blocks[me, :, at : at + LANES] = (real * factor).astype(jnp.bfloat16)
        blocks[me, :, length + at : length + at + LANES] = (imag * factor).astype(jnp.bfloat16)

    pl.semaphore_wait(barrier, 3)

    for h in (0, 1):
        ring(0, 0, h).start()
        ring(1, 0, 1 - h).start()
    for h in (0, 1):
        pair(0, 0, h).start()

    def modulate(lag, carry):
        cosine = tables[0, pl.ds(lag, 1), :]
        sine = tables[1, pl.ds(lag, 1), :]
        rows = pl.ds(pl.multiple_of(lag * members, members), members)
        for at in range(0, length, LANES):
            real = blocks[me, :, at : at + LANES].astype(jnp.float32)
            imag = blocks[me, :, length + at : length + at + LANES].astype(jnp.float32)
            modulated[rows, at : at + LANES] = (cosine * real - sine * imag).astype(jnp.bfloat16)
            modulated[rows, length + at : length + at + LANES] = (
                cosine * imag + sine * real
            ).astype(jnp.bfloat16)
        return carry

    lax.fori_loop(0, lag_count, modulate, 0)

    def correlate(way, distance):
        tile = source_chip(way, distance)
        others = blocks[pl.ds(tile * 2, 2)].reshape(2 * members, 2 * length)
        sums = lax.dot_general(
            modulated[...], others, (((1,), (1,)), ((), ())),
            preferred_element_type=jnp.float32,
        )
        width = 2 * members
        columns = pl.ds(pl.multiple_of(tile * width, width), width)
        out[:, :, columns] = sums.reshape(lag_count, members, width)

    def pair_ready(way, distance):
        for h in (0, 1):
            pair(way, distance, h, incoming=True).wait_recv()

    def take(step, h, last):
        for way in (0, 1):
            part = h if way == 0 else 1 - h
            ring(way, step - 1, part, incoming=True).wait_recv()
            if not last or h == 0:
                ring(way, step, part).start()
            pair(way, step, part).start()

    take(1, 0, far == 2)
    pair_ready(0, 0)
    correlate(0, 0)
    take(1, 1, far == 2)

    def onward(step, last):
        take(step, 0, last)
        pair_ready(0, step - 1)
        correlate(0, step - 1)
        take(step, 1, last)
        pair_ready(1, step - 1)
        correlate(1, step - 1)

    def body(step, carry):
        onward(step, False)
        return carry

    lax.fori_loop(2, far - 1, body, 0)
    onward(far - 1, True)

    pair_ready(0, far - 1)
    correlate(0, far - 1)
    pair_ready(1, far - 1)
    for way in (0, 1):
        ring(way, far - 1, way, incoming=True).wait_recv()
        pair(way, far, way).start()
    correlate(1, far - 1)
    for way in (0, 1):
        pair(way, far, way, incoming=True).wait_recv()
    correlate(0, far)

    def drain(step, carry):
        for way in (0, 1):
            for h in (0, 1):
                ring(way, step, h).wait_send()
                pair(way, step + 1, h).wait_send()
        return carry

    lax.fori_loop(0, far - 1, drain, 0)
    for way in (0, 1):
        ring(way, far - 1, way).wait_send()
        pair(way, far, way).wait_send()
    for h in (0, 1):
        pair(0, 0, h).wait_send()


def per_device(spectra, gap_mask):
    devices = lax.axis_size("blk")
    members, length = spectra.shape[1], spectra.shape[2]
    far = devices // 4
    tables = phase_tables(length // gap_mask.shape[1], LAGS, 1.0 / math.sqrt(length))
    return pl.pallas_call(
        functools.partial(kernel, devices),
        out_shape=jax.ShapeDtypeStruct((LAGS, members, devices * members), jnp.float32),
        in_specs=[pl.BlockSpec(memory_space=pltpu.VMEM)] * 3,
        out_specs=pl.BlockSpec(memory_space=pltpu.VMEM),
        scratch_shapes=[
            pltpu.VMEM((devices, members, 2 * length), jnp.bfloat16),
            pltpu.VMEM((LAGS * members, 2 * length), jnp.bfloat16),
            pltpu.SemaphoreType.DMA((2, far, 2)),
            pltpu.SemaphoreType.DMA((2, far, 2)),
            pltpu.SemaphoreType.DMA((2, far + 1, 2)),
            pltpu.SemaphoreType.DMA((2, far + 1, 2)),
        ],
        compiler_params=pltpu.CompilerParams(
            collective_id=0, has_side_effects=True, vmem_limit_bytes=60 * 1024 * 1024
        ),
    )(spectra, gap_mask.T, jnp.asarray(tables))


def solution(mesh):
    placed = (P(None, ("group", "blk"), None), P(("group", "blk"), None))
    return jax.shard_map(
        per_device,
        mesh=mesh,
        in_specs=placed,
        out_specs=P(None, ("group", "blk"), None),
        check_vma=False,
    )
```

```python
import functools
import math

import jax
import jax.numpy as jnp
import numpy as np
from jax import lax
from jax.experimental import pallas as pl
from jax.experimental.pallas import tpu as pltpu
from jax.sharding import PartitionSpec as P

LAGS = 8
LANES = 128
level_floor = 0.3
first_bin = 96.0
reach = 2


def phase_tables(bin_count, lag_count, scale):
    freq = first_bin + np.arange(bin_count, dtype=np.float32)
    shifts = 3.0 + 5.0 * np.arange(lag_count, dtype=np.float32)
    theta = np.float32(2.0 * math.pi) * freq[None, :] * shifts[:, None] / np.float32(512.0)
    tables = np.stack([np.cos(theta), np.sin(theta)]) * np.float32(scale)
    return np.tile(tables, (1, 1, LANES // bin_count)).astype(np.float32)


def ring_chip(chips, position):
    position = (position + 2 * chips) % chips
    return jnp.where(position < (chips + 1) // 2, 2 * position, 2 * chips - 1 - 2 * position)


def ring_spot(chips, chip):
    return jnp.where(chip % 2 == 0, chip // 2, chips - 1 - chip // 2)


def tile_product(modulated, blocks, tile, lag_count):
    _, members, depth = blocks.shape
    others = blocks[pl.ds(tile * 2, 2)].reshape(2 * members, depth)
    sums = lax.dot_general(
        modulated[...], others, (((1,), (1,)), ((), ())), preferred_element_type=jnp.float32
    )
    return sums.reshape(lag_count, members, 2 * members)


def finish(devices, partial, blocks, modulated, out, last, done):
    chips = devices // 2
    lag_count, members = partial.shape[0], partial.shape[1]
    width = 2 * members
    spot = ring_spot(chips, lax.axis_index("blk") // 2)
    far_tile = ring_chip(chips, spot + chips // 2)

    def columns(tile):
        return pl.ds(pl.multiple_of(tile * width, width), width)

    def place(away):
        cut = columns(ring_chip(chips, spot + chips // 2 + away))
        return pltpu.make_async_copy(partial.at[:, :, cut], out.at[:, :, cut], done.at[away])

    def begin(away, carry):
        place(away).start()
        return carry

    def end(away, carry):
        place(away).wait()
        return carry

    lax.fori_loop(1, chips, begin, 0)
    last[...] = tile_product(modulated, blocks, far_tile, lag_count)
    tail = pltpu.make_async_copy(last, out.at[:, :, columns(far_tile)], done.at[0])
    tail.start()
    lax.fori_loop(1, chips, end, 0)
    tail.wait()


def kernel(
    devices, spectra, gaps, tables, out, blocks, modulated,
    ring_send, ring_recv, pair_send, pair_recv,
):
    members, length = spectra.shape[1], spectra.shape[2]
    windows = gaps.shape[0]
    bins = length // windows
    lag_count = out.shape[0]
    half = members // 2
    chips = devices // 2
    far = chips // 2

    me = lax.axis_index("blk")
    chip, core = me // 2, me % 2
    spot = ring_spot(chips, chip)

    def chip_at(position):
        return ring_chip(chips, position)

    targets = (chip_at(spot + 1) * 2 + core, chip_at(spot - 1) * 2 + core)
    partner = chip * 2 + (1 - core)

    def source_chip(way, distance):
        return chip_at(spot - distance if way == 0 else spot + distance)

    def piece(block, h):
        return blocks.at[block, pl.ds(h * half, half), :]

    def ring(way, step, h, incoming=False):
        place = piece(source_chip(way, step + 1 if incoming else step) * 2 + core, h)
        return pltpu.make_async_remote_copy(
            src_ref=place, dst_ref=place,
            send_sem=ring_send.at[way, step, h], recv_sem=ring_recv.at[way, step, h],
            device_id={"blk": targets[way]}, device_id_type=pl.DeviceIdType.MESH,
        )

    def pair(way, distance, h, incoming=False):
        side = 1 - core if incoming else core
        place = piece(source_chip(way, distance) * 2 + side, h)
        return pltpu.make_async_remote_copy(
            src_ref=place, dst_ref=place,
            send_sem=pair_send.at[way, distance, h], recv_sem=pair_recv.at[way, distance, h],
            device_id={"blk": partner}, device_id_type=pl.DeviceIdType.MESH,
        )

    barrier = pltpu.get_barrier_semaphore()
    for other in (*targets, partner):
        pl.semaphore_signal(
            barrier, inc=1, device_id={"blk": other}, device_id_type=pl.DeviceIdType.MESH
        )

    window_of = lax.broadcasted_iota(jnp.int32, (windows, length), 1) // bins
    spread = window_of == lax.broadcasted_iota(jnp.int32, (windows, length), 0)
    live = lax.dot_general(
        gaps[...].astype(jnp.float32).astype(jnp.bfloat16),
        spread.astype(jnp.float32).astype(jnp.bfloat16),
        (((0,), (0,)), ((), ())),
        preferred_element_type=jnp.float32,
    )
    bin_of = lax.broadcasted_iota(jnp.int32, (members, LANES), 1) % bins
    count = 1 + jnp.minimum(bin_of, reach) + jnp.minimum(bins - 1 - bin_of, reach)
    weight = 1.0 / count.astype(jnp.float32)
    for at in range(0, length, LANES):
        cut = slice(at, at + LANES)
        real = spectra[0, :, cut].astype(jnp.float32)
        imag = spectra[1, :, cut].astype(jnp.float32)
        amplitude = jnp.sqrt(real * real + imag * imag)
        total = amplitude
        for off in range(1, reach + 1):
            total += jnp.where(bin_of >= off, pltpu.roll(amplitude, off, 1), 0.0)
            total += jnp.where(bin_of < bins - off, pltpu.roll(amplitude, LANES - off, 1), 0.0)
        level = jnp.maximum(total * weight, level_floor)
        factor = live[:, cut] / level
        blocks[me, :, at : at + LANES] = (real * factor).astype(jnp.bfloat16)
        blocks[me, :, length + at : length + at + LANES] = (imag * factor).astype(jnp.bfloat16)

    pl.semaphore_wait(barrier, 3)

    for h in (0, 1):
        ring(0, 0, h).start()
        ring(1, 0, 1 - h).start()
    for h in (0, 1):
        pair(0, 0, h).start()

    def modulate(lag, carry):
        cosine = tables[0, pl.ds(lag, 1), :]
        sine = tables[1, pl.ds(lag, 1), :]
        rows = pl.ds(pl.multiple_of(lag * members, members), members)
        for at in range(0, length, LANES):
            real = blocks[me, :, at : at + LANES].astype(jnp.float32)
            imag = blocks[me, :, length + at : length + at + LANES].astype(jnp.float32)
            modulated[rows, at : at + LANES] = (cosine * real - sine * imag).astype(jnp.bfloat16)
            modulated[rows, length + at : length + at + LANES] = (
                cosine * imag + sine * real
            ).astype(jnp.bfloat16)
        return carry

    lax.fori_loop(0, lag_count, modulate, 0)

    def correlate(way, distance):
        tile = source_chip(way, distance)
        width = 2 * members
        columns = pl.ds(pl.multiple_of(tile * width, width), width)
        out[:, :, columns] = tile_product(modulated, blocks, tile, lag_count)

    def pair_ready(way, distance):
        for h in (0, 1):
            pair(way, distance, h, incoming=True).wait_recv()

    def take(step, h, last):
        for way in (0, 1):
            part = h if way == 0 else 1 - h
            ring(way, step - 1, part, incoming=True).wait_recv()
            if not last or h == 0:
                ring(way, step, part).start()
            pair(way, step, part).start()

    take(1, 0, far == 2)
    pair_ready(0, 0)
    correlate(0, 0)
    take(1, 1, far == 2)

    def onward(step, last):
        take(step, 0, last)
        pair_ready(0, step - 1)
        correlate(0, step - 1)
        take(step, 1, last)
        pair_ready(1, step - 1)
        correlate(1, step - 1)

    def body(step, carry):
        onward(step, False)
        return carry

    lax.fori_loop(2, far - 1, body, 0)
    onward(far - 1, True)

    pair_ready(0, far - 1)
    correlate(0, far - 1)
    pair_ready(1, far - 1)
    for way in (0, 1):
        ring(way, far - 1, way, incoming=True).wait_recv()
        pair(way, far, way).start()
    correlate(1, far - 1)
    for way in (0, 1):
        pair(way, far, way, incoming=True).wait_recv()

    def drain(step, carry):
        for way in (0, 1):
            for h in (0, 1):
                ring(way, step, h).wait_send()
                pair(way, step + 1, h).wait_send()
        return carry

    lax.fori_loop(0, far - 1, drain, 0)
    for way in (0, 1):
        ring(way, far - 1, way).wait_send()
        pair(way, far, way).wait_send()
    for h in (0, 1):
        pair(0, 0, h).wait_send()


def per_device(spectra, gap_mask):
    devices = lax.axis_size("blk")
    members, length = spectra.shape[1], spectra.shape[2]
    far = devices // 4
    tables = phase_tables(length // gap_mask.shape[1], LAGS, 1.0 / math.sqrt(length))
    result = (LAGS, members, devices * members)
    vmem = pl.BlockSpec(memory_space=pltpu.VMEM)
    partial, blocks, modulated = pl.pallas_call(
        functools.partial(kernel, devices),
        out_shape=[
            pltpu.VMEM(result, jnp.float32),
            pltpu.VMEM((devices, members, 2 * length), jnp.bfloat16),
            pltpu.VMEM((LAGS * members, 2 * length), jnp.bfloat16),
        ],
        in_specs=[vmem] * 3,
        out_specs=[vmem] * 3,
        scratch_shapes=[
            pltpu.SemaphoreType.DMA((2, far, 2)),
            pltpu.SemaphoreType.DMA((2, far, 2)),
            pltpu.SemaphoreType.DMA((2, far + 1, 2)),
            pltpu.SemaphoreType.DMA((2, far + 1, 2)),
        ],
        compiler_params=pltpu.CompilerParams(
            collective_id=0, has_side_effects=True, vmem_limit_bytes=16 * 1024 * 1024
        ),
    )(spectra, gap_mask.T, jnp.asarray(tables))
    return pl.pallas_call(
        functools.partial(finish, devices),
        out_shape=jax.ShapeDtypeStruct(result, jnp.float32),
        in_specs=[vmem] * 3,
        out_specs=pl.BlockSpec(memory_space=pl.ANY),
        scratch_shapes=[
            pltpu.VMEM((LAGS, members, 2 * members), jnp.float32),
            pltpu.SemaphoreType.DMA((devices // 2,)),
        ],
        compiler_params=pltpu.CompilerParams(vmem_limit_bytes=16 * 1024 * 1024),
    )(partial, blocks, modulated)


def solution(mesh):
    placed = (P(None, ("group", "blk"), None), P(("group", "blk"), None))
    return jax.shard_map(
        per_device,
        mesh=mesh,
        in_specs=placed,
        out_specs=P(None, ("group", "blk"), None),
        check_vma=False,
    )
```

```python
import functools
import math

import jax
import jax.numpy as jnp
import numpy as np
from jax import lax
from jax.experimental import pallas as pl
from jax.experimental.pallas import tpu as pltpu
from jax.sharding import PartitionSpec as P

LAGS = 8
LANES = 128
level_floor = 0.3
first_bin = 96.0
reach = 2


def phase_tables(bin_count, lag_count, scale):
    freq = first_bin + np.arange(bin_count, dtype=np.float32)
    shifts = 3.0 + 5.0 * np.arange(lag_count, dtype=np.float32)
    theta = np.float32(2.0 * math.pi) * freq[None, :] * shifts[:, None] / np.float32(512.0)
    tables = np.stack([np.cos(theta), np.sin(theta)]) * np.float32(scale)
    return np.tile(tables, (1, 1, LANES // bin_count)).astype(np.float32)


def ring_chip(chips, position):
    position = (position + 2 * chips) % chips
    return jnp.where(position < (chips + 1) // 2, 2 * position, 2 * chips - 1 - 2 * position)


def ring_spot(chips, chip):
    return jnp.where(chip % 2 == 0, chip // 2, chips - 1 - chip // 2)


def tile_product(modulated, blocks, tile, lag_count):
    _, members, depth = blocks.shape
    others = blocks[pl.ds(tile * 2, 2)].reshape(2 * members, depth)
    sums = lax.dot_general(
        modulated[...], others, (((1,), (1,)), ((), ())), preferred_element_type=jnp.float32
    )
    return sums.reshape(lag_count, members, 2 * members)


def finish(devices, partial, blocks, modulated, out, last, done):
    chips = devices // 2
    lag_count, members = partial.shape[0], partial.shape[1]
    width = 2 * members
    spot = ring_spot(chips, lax.axis_index("blk") // 2)
    far_tile = ring_chip(chips, spot + chips // 2)

    def columns(tile):
        return pl.ds(pl.multiple_of(tile * width, width), width)

    def place(away):
        cut = columns(ring_chip(chips, spot + chips // 2 + away))
        return pltpu.make_async_copy(partial.at[:, :, cut], out.at[:, :, cut], done.at[away])

    def begin(away, carry):
        place(away).start()
        return carry

    def end(away, carry):
        place(away).wait()
        return carry

    lax.fori_loop(1, chips, begin, 0)
    last[...] = tile_product(modulated, blocks, far_tile, lag_count)
    tail = pltpu.make_async_copy(last, out.at[:, :, columns(far_tile)], done.at[0])
    tail.start()
    lax.fori_loop(1, chips, end, 0)
    tail.wait()


def kernel(
    devices, spectra_in, gaps_in, tables_in, out, blocks, modulated,
    spectra, gaps, tables, fetched, ring_send, ring_recv, pair_send, pair_recv,
):
    members, length = spectra.shape[1], spectra.shape[2]
    windows = gaps.shape[0]
    bins = length // windows
    lag_count = out.shape[0]
    half = members // 2
    chips = devices // 2
    far = chips // 2

    me = lax.axis_index("blk")
    chip, core = me // 2, me % 2
    spot = ring_spot(chips, chip)

    def chip_at(position):
        return ring_chip(chips, position)

    targets = (chip_at(spot + 1) * 2 + core, chip_at(spot - 1) * 2 + core)
    partner = chip * 2 + (1 - core)

    def source_chip(way, distance):
        return chip_at(spot - distance if way == 0 else spot + distance)

    def piece(block, h):
        return blocks.at[block, pl.ds(h * half, half), :]

    def ring(way, step, h, incoming=False):
        place = piece(source_chip(way, step + 1 if incoming else step) * 2 + core, h)
        return pltpu.make_async_remote_copy(
            src_ref=place, dst_ref=place,
            send_sem=ring_send.at[way, step, h], recv_sem=ring_recv.at[way, step, h],
            device_id={"blk": targets[way]}, device_id_type=pl.DeviceIdType.MESH,
        )

    def pair(way, distance, h, incoming=False):
        side = 1 - core if incoming else core
        place = piece(source_chip(way, distance) * 2 + side, h)
        return pltpu.make_async_remote_copy(
            src_ref=place, dst_ref=place,
            send_sem=pair_send.at[way, distance, h], recv_sem=pair_recv.at[way, distance, h],
            device_id={"blk": partner}, device_id_type=pl.DeviceIdType.MESH,
        )

    fetches = [
        pltpu.make_async_copy(source, place, fetched.at[i])
        for i, (source, place) in enumerate(
            ((gaps_in, gaps), (spectra_in, spectra), (tables_in, tables))
        )
    ]
    for fetch in fetches:
        fetch.start()

    barrier = pltpu.get_barrier_semaphore()
    for other in (*targets, partner):
        pl.semaphore_signal(
            barrier, inc=1, device_id={"blk": other}, device_id_type=pl.DeviceIdType.MESH
        )

    window_of = lax.broadcasted_iota(jnp.int32, (windows, length), 1) // bins
    spread = window_of == lax.broadcasted_iota(jnp.int32, (windows, length), 0)
    bin_of = lax.broadcasted_iota(jnp.int32, (half, LANES), 1) % bins
    count = 1 + jnp.minimum(bin_of, reach) + jnp.minimum(bins - 1 - bin_of, reach)
    weight = 1.0 / count.astype(jnp.float32)
    fetches[0].wait()
    live = lax.dot_general(
        gaps[...].astype(jnp.float32).astype(jnp.bfloat16),
        spread.astype(jnp.float32).astype(jnp.bfloat16),
        (((0,), (0,)), ((), ())),
        preferred_element_type=jnp.float32,
    )
    fetches[1].wait()

    def whiten(h):
        rows = slice(h * half, (h + 1) * half)
        for at in range(0, length, LANES):
            cut = slice(at, at + LANES)
            real = spectra[0, rows, cut].astype(jnp.float32)
            imag = spectra[1, rows, cut].astype(jnp.float32)
            amplitude = jnp.sqrt(real * real + imag * imag)
            total = amplitude
            for off in range(1, reach + 1):
                total += jnp.where(bin_of >= off, pltpu.roll(amplitude, off, 1), 0.0)
                total += jnp.where(bin_of < bins - off, pltpu.roll(amplitude, LANES - off, 1), 0.0)
            level = jnp.maximum(total * weight, level_floor)
            factor = live[rows, cut] / level
            blocks[me, rows, at : at + LANES] = (real * factor).astype(jnp.bfloat16)
            blocks[me, rows, length + at : length + at + LANES] = (imag * factor).astype(
                jnp.bfloat16
            )

    whiten(0)
    pl.semaphore_wait(barrier, 3)
    ring(0, 0, 0).start()
    whiten(1)
    ring(1, 0, 1).start()
    ring(0, 0, 1).start()
    ring(1, 0, 0).start()
    for h in (0, 1):
        pair(0, 0, h).start()
    fetches[2].wait()

    def modulate(lag, carry):
        cosine = tables[0, pl.ds(lag, 1), :]
        sine = tables[1, pl.ds(lag, 1), :]
        rows = pl.ds(pl.multiple_of(lag * members, members), members)
        for at in range(0, length, LANES):
            real = blocks[me, :, at : at + LANES].astype(jnp.float32)
            imag = blocks[me, :, length + at : length + at + LANES].astype(jnp.float32)
            modulated[rows, at : at + LANES] = (cosine * real - sine * imag).astype(jnp.bfloat16)
            modulated[rows, length + at : length + at + LANES] = (
                cosine * imag + sine * real
            ).astype(jnp.bfloat16)
        return carry

    lax.fori_loop(0, lag_count, modulate, 0)

    def correlate(way, distance):
        tile = source_chip(way, distance)
        width = 2 * members
        columns = pl.ds(pl.multiple_of(tile * width, width), width)
        out[:, :, columns] = tile_product(modulated, blocks, tile, lag_count)

    def pair_ready(way, distance):
        for h in (0, 1):
            pair(way, distance, h, incoming=True).wait_recv()

    def take(step, h, last):
        for way in (0, 1):
            part = h if way == 0 else 1 - h
            ring(way, step - 1, part, incoming=True).wait_recv()
            if not last or h == 0:
                ring(way, step, part).start()
            pair(way, step, part).start()

    take(1, 0, far == 2)
    pair_ready(0, 0)
    correlate(0, 0)
    take(1, 1, far == 2)

    def onward(step, last):
        take(step, 0, last)
        pair_ready(0, step - 1)
        correlate(0, step - 1)
        take(step, 1, last)
        pair_ready(1, step - 1)
        correlate(1, step - 1)

    def body(step, carry):
        onward(step, False)
        return carry

    lax.fori_loop(2, far - 1, body, 0)
    onward(far - 1, True)

    pair_ready(0, far - 1)
    correlate(0, far - 1)
    pair_ready(1, far - 1)
    for way in (0, 1):
        ring(way, far - 1, way, incoming=True).wait_recv()
        pair(way, far, way).start()
    correlate(1, far - 1)
    for way in (0, 1):
        pair(way, far, way, incoming=True).wait_recv()

    def drain(step, carry):
        for way in (0, 1):
            for h in (0, 1):
                ring(way, step, h).wait_send()
                pair(way, step + 1, h).wait_send()
        return carry

    lax.fori_loop(0, far - 1, drain, 0)
    for way in (0, 1):
        ring(way, far - 1, way).wait_send()
        pair(way, far, way).wait_send()
    for h in (0, 1):
        pair(0, 0, h).wait_send()


def per_device(spectra, gap_mask):
    devices = lax.axis_size("blk")
    members, length = spectra.shape[1], spectra.shape[2]
    far = devices // 4
    tables = phase_tables(length // gap_mask.shape[1], LAGS, 1.0 / math.sqrt(length))
    result = (LAGS, members, devices * members)
    vmem = pl.BlockSpec(memory_space=pltpu.VMEM)
    partial, blocks, modulated = pl.pallas_call(
        functools.partial(kernel, devices),
        out_shape=[
            pltpu.VMEM(result, jnp.float32),
            pltpu.VMEM((devices, members, 2 * length), jnp.bfloat16),
            pltpu.VMEM((LAGS * members, 2 * length), jnp.bfloat16),
        ],
        in_specs=[pl.BlockSpec(memory_space=pltpu.HBM)] * 3,
        out_specs=[vmem] * 3,
        scratch_shapes=[
            pltpu.VMEM(spectra.shape, spectra.dtype),
            pltpu.VMEM(gap_mask.shape[::-1], gap_mask.dtype),
            pltpu.VMEM(tables.shape, jnp.float32),
            pltpu.SemaphoreType.DMA((3,)),
            pltpu.SemaphoreType.DMA((2, far, 2)),
            pltpu.SemaphoreType.DMA((2, far, 2)),
            pltpu.SemaphoreType.DMA((2, far + 1, 2)),
            pltpu.SemaphoreType.DMA((2, far + 1, 2)),
        ],
        compiler_params=pltpu.CompilerParams(
            collective_id=0, has_side_effects=True, vmem_limit_bytes=16 * 1024 * 1024
        ),
    )(spectra, gap_mask.T, jnp.asarray(tables))
    return pl.pallas_call(
        functools.partial(finish, devices),
        out_shape=jax.ShapeDtypeStruct(result, jnp.float32),
        in_specs=[vmem] * 3,
        out_specs=pl.BlockSpec(memory_space=pl.ANY),
        scratch_shapes=[
            pltpu.VMEM((LAGS, members, 2 * members), jnp.float32),
            pltpu.SemaphoreType.DMA((devices // 2,)),
        ],
        compiler_params=pltpu.CompilerParams(vmem_limit_bytes=16 * 1024 * 1024),
    )(partial, blocks, modulated)


def solution(mesh):
    placed = (P(None, ("group", "blk"), None), P(("group", "blk"), None))
    return jax.shard_map(
        per_device,
        mesh=mesh,
        in_specs=placed,
        out_specs=P(None, ("group", "blk"), None),
        check_vma=False,
    )
```

```python
import functools
import math

import jax
import jax.numpy as jnp
import numpy as np
from jax import lax
from jax.experimental import pallas as pl
from jax.experimental.pallas import tpu as pltpu
from jax.sharding import PartitionSpec as P

LAGS = 8
LANES = 128
VMEM_BYTES = 67043328
level_floor = 0.3
first_bin = 96.0
reach = 2


def phase_tables(bin_count, lag_count, scale):
    freq = first_bin + np.arange(bin_count, dtype=np.float32)
    shifts = 3.0 + 5.0 * np.arange(lag_count, dtype=np.float32)
    theta = np.float32(2.0 * math.pi) * freq[None, :] * shifts[:, None] / np.float32(512.0)
    tables = np.stack([np.cos(theta), np.sin(theta)]) * np.float32(scale)
    return np.tile(tables, (1, 1, LANES // bin_count)).astype(np.float32)


def ring_chip(chips, position):
    position = (position + 2 * chips) % chips
    return jnp.where(position < (chips + 1) // 2, 2 * position, 2 * chips - 1 - 2 * position)


def ring_spot(chips, chip):
    return jnp.where(chip % 2 == 0, chip // 2, chips - 1 - chip // 2)


def tile_product(modulated, blocks, tile, lag_count):
    _, members, depth = blocks.shape
    others = blocks[pl.ds(tile * 2, 2)].reshape(2 * members, depth)
    sums = lax.dot_general(
        modulated[...], others, (((1,), (1,)), ((), ())), preferred_element_type=jnp.float32
    )
    return sums.reshape(lag_count, members, 2 * members)


def finish(devices, partial, blocks, modulated, out, last, done):
    chips = devices // 2
    lag_count, members = partial.shape[0], partial.shape[1]
    width = 2 * members
    spot = ring_spot(chips, lax.axis_index("blk") // 2)
    far_tile = ring_chip(chips, spot + chips // 2)

    def columns(tile):
        return pl.ds(pl.multiple_of(tile * width, width), width)

    def place(away):
        cut = columns(ring_chip(chips, spot + chips // 2 + away))
        return pltpu.make_async_copy(partial.at[:, :, cut], out.at[:, :, cut], done.at[away])

    def begin(away, carry):
        place(away).start()
        return carry

    def end(away, carry):
        place(away).wait()
        return carry

    lax.fori_loop(1, chips, begin, 0)
    last[...] = tile_product(modulated, blocks, far_tile, lag_count)
    tail = pltpu.make_async_copy(last, out.at[:, :, columns(far_tile)], done.at[0])
    tail.start()
    lax.fori_loop(1, chips, end, 0)
    tail.wait()


def kernel(
    devices, spectra_in, gaps_in, tables_in, out, blocks, modulated,
    spectra, gaps, tables, fetched, ring_send, ring_recv, pair_send, pair_recv,
):
    members, length = spectra.shape[1], spectra.shape[2]
    windows = gaps.shape[0]
    bins = length // windows
    lag_count = out.shape[0]
    half = members // 2
    chips = devices // 2
    far = chips // 2

    me = lax.axis_index("blk")
    chip, core = me // 2, me % 2
    spot = ring_spot(chips, chip)

    def chip_at(position):
        return ring_chip(chips, position)

    targets = (chip_at(spot + 1) * 2 + core, chip_at(spot - 1) * 2 + core)
    partner = chip * 2 + (1 - core)

    def source_chip(way, distance):
        return chip_at(spot - distance if way == 0 else spot + distance)

    def piece(block, h):
        return blocks.at[block, pl.ds(h * half, half), :]

    def ring(way, step, h, incoming=False):
        place = piece(source_chip(way, step + 1 if incoming else step) * 2 + core, h)
        return pltpu.make_async_remote_copy(
            src_ref=place, dst_ref=place,
            send_sem=ring_send.at[way, step, h], recv_sem=ring_recv.at[way, step, h],
            device_id={"blk": targets[way]}, device_id_type=pl.DeviceIdType.MESH,
        )

    def pair(way, distance, h, incoming=False):
        side = 1 - core if incoming else core
        place = piece(source_chip(way, distance) * 2 + side, h)
        return pltpu.make_async_remote_copy(
            src_ref=place, dst_ref=place,
            send_sem=pair_send.at[way, distance, h], recv_sem=pair_recv.at[way, distance, h],
            device_id={"blk": partner}, device_id_type=pl.DeviceIdType.MESH,
        )

    fetches = [
        pltpu.make_async_copy(source, place, fetched.at[i])
        for i, (source, place) in enumerate(
            ((gaps_in, gaps), (spectra_in, spectra), (tables_in, tables))
        )
    ]
    for fetch in fetches:
        fetch.start()

    barrier = pltpu.get_barrier_semaphore()
    for other in (*targets, partner):
        pl.semaphore_signal(
            barrier, inc=1, device_id={"blk": other}, device_id_type=pl.DeviceIdType.MESH
        )

    window_of = lax.broadcasted_iota(jnp.int32, (windows, length), 1) // bins
    spread = window_of == lax.broadcasted_iota(jnp.int32, (windows, length), 0)
    bin_of = lax.broadcasted_iota(jnp.int32, (half, LANES), 1) % bins
    count = 1 + jnp.minimum(bin_of, reach) + jnp.minimum(bins - 1 - bin_of, reach)
    weight = 1.0 / count.astype(jnp.float32)
    fetches[0].wait()
    live = lax.dot_general(
        gaps[...].astype(jnp.float32).astype(jnp.bfloat16),
        spread.astype(jnp.float32).astype(jnp.bfloat16),
        (((0,), (0,)), ((), ())),
        preferred_element_type=jnp.float32,
    )
    fetches[1].wait()

    def whiten(h):
        rows = slice(h * half, (h + 1) * half)
        for at in range(0, length, LANES):
            cut = slice(at, at + LANES)
            real = spectra[0, rows, cut].astype(jnp.float32)
            imag = spectra[1, rows, cut].astype(jnp.float32)
            amplitude = jnp.sqrt(real * real + imag * imag)
            total = amplitude
            for off in range(1, reach + 1):
                total += jnp.where(bin_of >= off, pltpu.roll(amplitude, off, 1), 0.0)
                total += jnp.where(bin_of < bins - off, pltpu.roll(amplitude, LANES - off, 1), 0.0)
            level = jnp.maximum(total * weight, level_floor)
            factor = live[rows, cut] / level
            blocks[me, rows, at : at + LANES] = (real * factor).astype(jnp.bfloat16)
            blocks[me, rows, length + at : length + at + LANES] = (imag * factor).astype(
                jnp.bfloat16
            )

    whiten(0)
    pl.semaphore_wait(barrier, 3)
    ring(0, 0, 0).start()
    whiten(1)
    ring(1, 0, 1).start()
    ring(0, 0, 1).start()
    ring(1, 0, 0).start()
    for h in (0, 1):
        pair(0, 0, h).start()
    fetches[2].wait()

    def modulate(lag, carry):
        cosine = tables[0, pl.ds(lag, 1), :]
        sine = tables[1, pl.ds(lag, 1), :]
        rows = pl.ds(pl.multiple_of(lag * members, members), members)
        for at in range(0, length, LANES):
            real = blocks[me, :, at : at + LANES].astype(jnp.float32)
            imag = blocks[me, :, length + at : length + at + LANES].astype(jnp.float32)
            modulated[rows, at : at + LANES] = (cosine * real - sine * imag).astype(jnp.bfloat16)
            modulated[rows, length + at : length + at + LANES] = (
                cosine * imag + sine * real
            ).astype(jnp.bfloat16)
        return carry

    lax.fori_loop(0, lag_count, modulate, 0)

    def correlate(way, distance):
        tile = source_chip(way, distance)
        width = 2 * members
        columns = pl.ds(pl.multiple_of(tile * width, width), width)
        out[:, :, columns] = tile_product(modulated, blocks, tile, lag_count)

    def pair_ready(way, distance):
        for h in (0, 1):
            pair(way, distance, h, incoming=True).wait_recv()

    def take(step, h, last):
        for way in (0, 1):
            part = h if way == 0 else 1 - h
            ring(way, step - 1, part, incoming=True).wait_recv()
            if not last or h == 0:
                ring(way, step, part).start()
            pair(way, step, part).start()

    take(1, 0, far == 2)
    pair_ready(0, 0)
    correlate(0, 0)
    take(1, 1, far == 2)

    def onward(step, last):
        take(step, 0, last)
        pair_ready(0, step - 1)
        correlate(0, step - 1)
        take(step, 1, last)
        pair_ready(1, step - 1)
        correlate(1, step - 1)

    def body(step, carry):
        onward(step, False)
        return carry

    lax.fori_loop(2, far - 1, body, 0)
    onward(far - 1, True)

    pair_ready(0, far - 1)
    correlate(0, far - 1)
    pair_ready(1, far - 1)
    for way in (0, 1):
        ring(way, far - 1, way, incoming=True).wait_recv()
        pair(way, far, way).start()
    correlate(1, far - 1)
    for way in (0, 1):
        pair(way, far, way, incoming=True).wait_recv()

    def drain(step, carry):
        for way in (0, 1):
            for h in (0, 1):
                ring(way, step, h).wait_send()
                pair(way, step + 1, h).wait_send()
        return carry

    lax.fori_loop(0, far - 1, drain, 0)
    for way in (0, 1):
        ring(way, far - 1, way).wait_send()
        pair(way, far, way).wait_send()
    for h in (0, 1):
        pair(0, 0, h).wait_send()


def per_device(spectra, gap_mask):
    devices = lax.axis_size("blk")
    members, length = spectra.shape[1], spectra.shape[2]
    far = devices // 4
    tables = phase_tables(length // gap_mask.shape[1], LAGS, 1.0 / math.sqrt(length))
    result = (LAGS, members, devices * members)
    kept = 4 * math.prod(result) + 4 * (devices + LAGS) * members * length
    vmem = pl.BlockSpec(memory_space=pltpu.VMEM)
    partial, blocks, modulated = pl.pallas_call(
        functools.partial(kernel, devices),
        out_shape=[
            pltpu.VMEM(result, jnp.float32),
            pltpu.VMEM((devices, members, 2 * length), jnp.bfloat16),
            pltpu.VMEM((LAGS * members, 2 * length), jnp.bfloat16),
        ],
        in_specs=[pl.BlockSpec(memory_space=pltpu.HBM)] * 3,
        out_specs=[vmem] * 3,
        scratch_shapes=[
            pltpu.VMEM(spectra.shape, spectra.dtype),
            pltpu.VMEM(gap_mask.shape[::-1], gap_mask.dtype),
            pltpu.VMEM(tables.shape, jnp.float32),
            pltpu.SemaphoreType.DMA((3,)),
            pltpu.SemaphoreType.DMA((2, far, 2)),
            pltpu.SemaphoreType.DMA((2, far, 2)),
            pltpu.SemaphoreType.DMA((2, far + 1, 2)),
            pltpu.SemaphoreType.DMA((2, far + 1, 2)),
        ],
        compiler_params=pltpu.CompilerParams(
            collective_id=0, has_side_effects=True, vmem_limit_bytes=VMEM_BYTES - kept
        ),
    )(spectra, gap_mask.T, jnp.asarray(tables))
    return pl.pallas_call(
        functools.partial(finish, devices),
        out_shape=jax.ShapeDtypeStruct(result, jnp.float32),
        in_specs=[vmem] * 3,
        out_specs=pl.BlockSpec(memory_space=pl.ANY),
        scratch_shapes=[
            pltpu.VMEM((LAGS, members, 2 * members), jnp.float32),
            pltpu.SemaphoreType.DMA((devices // 2,)),
        ],
        compiler_params=pltpu.CompilerParams(vmem_limit_bytes=16 * 1024 * 1024),
    )(partial, blocks, modulated)


def solution(mesh):
    placed = (P(None, ("group", "blk"), None), P(("group", "blk"), None))
    return jax.shard_map(
        per_device,
        mesh=mesh,
        in_specs=placed,
        out_specs=P(None, ("group", "blk"), None),
        check_vma=False,
    )
```

```python
import functools
import math

import jax
import jax.numpy as jnp
import numpy as np
from jax import lax
from jax.experimental import pallas as pl
from jax.experimental.pallas import tpu as pltpu
from jax.sharding import PartitionSpec as P

LAGS = 8
LANES = 128
PIECES = 4
VMEM_BYTES = 67043328
level_floor = 0.3
first_bin = 96.0
reach = 2


def phase_tables(bin_count, lag_count, scale):
    freq = first_bin + np.arange(bin_count, dtype=np.float32)
    shifts = 3.0 + 5.0 * np.arange(lag_count, dtype=np.float32)
    theta = np.float32(2.0 * math.pi) * freq[None, :] * shifts[:, None] / np.float32(512.0)
    tables = np.stack([np.cos(theta), np.sin(theta)]) * np.float32(scale)
    return np.tile(tables, (1, 1, LANES // bin_count)).astype(np.float32)


def ring_chip(chips, position):
    position = (position + 2 * chips) % chips
    return jnp.where(position < (chips + 1) // 2, 2 * position, 2 * chips - 1 - 2 * position)


def ring_spot(chips, chip):
    return jnp.where(chip % 2 == 0, chip // 2, chips - 1 - chip // 2)


def tile_product(modulated, blocks, tile, lag_count):
    _, members, depth = blocks.shape
    others = blocks[pl.ds(tile * 2, 2)].reshape(2 * members, depth)
    sums = lax.dot_general(
        modulated[...], others, (((1,), (1,)), ((), ())), preferred_element_type=jnp.float32
    )
    return sums.reshape(lag_count, members, 2 * members)


def finish(devices, partial, blocks, modulated, out, last, done):
    chips = devices // 2
    lag_count, members = partial.shape[0], partial.shape[1]
    width = 2 * members
    spot = ring_spot(chips, lax.axis_index("blk") // 2)
    far_tile = ring_chip(chips, spot + chips // 2)

    def columns(tile):
        return pl.ds(pl.multiple_of(tile * width, width), width)

    def place(away):
        cut = columns(ring_chip(chips, spot + chips // 2 + away))
        return pltpu.make_async_copy(partial.at[:, :, cut], out.at[:, :, cut], done.at[away])

    def begin(away, carry):
        place(away).start()
        return carry

    def end(away, carry):
        place(away).wait()
        return carry

    lax.fori_loop(1, chips, begin, 0)
    last[...] = tile_product(modulated, blocks, far_tile, lag_count)
    tail = pltpu.make_async_copy(last, out.at[:, :, columns(far_tile)], done.at[0])
    tail.start()
    lax.fori_loop(1, chips, end, 0)
    tail.wait()


def kernel(
    devices, spectra_in, gaps_in, tables_in, out, blocks, modulated,
    spectra, gaps, tables, fetched, ring_send, ring_recv, pair_send, pair_recv,
):
    members, length = spectra.shape[1], spectra.shape[2]
    windows = gaps.shape[0]
    bins = length // windows
    lag_count = out.shape[0]
    height = members // PIECES
    order = [[(i + way * PIECES // 2) % PIECES for i in range(PIECES)] for way in (0, 1)]
    chips = devices // 2
    far = chips // 2

    me = lax.axis_index("blk")
    chip, core = me // 2, me % 2
    spot = ring_spot(chips, chip)

    def chip_at(position):
        return ring_chip(chips, position)

    targets = (chip_at(spot + 1) * 2 + core, chip_at(spot - 1) * 2 + core)
    partner = chip * 2 + (1 - core)

    def source_chip(way, distance):
        return chip_at(spot - distance if way == 0 else spot + distance)

    def piece(block, h):
        return blocks.at[block, pl.ds(h * height, height), :]

    def ring(way, step, h, incoming=False):
        place = piece(source_chip(way, step + 1 if incoming else step) * 2 + core, h)
        return pltpu.make_async_remote_copy(
            src_ref=place, dst_ref=place,
            send_sem=ring_send.at[way, step, h], recv_sem=ring_recv.at[way, step, h],
            device_id={"blk": targets[way]}, device_id_type=pl.DeviceIdType.MESH,
        )

    def pair(way, distance, h, incoming=False):
        side = 1 - core if incoming else core
        place = piece(source_chip(way, distance) * 2 + side, h)
        return pltpu.make_async_remote_copy(
            src_ref=place, dst_ref=place,
            send_sem=pair_send.at[way, distance, h], recv_sem=pair_recv.at[way, distance, h],
            device_id={"blk": partner}, device_id_type=pl.DeviceIdType.MESH,
        )

    fetches = [
        pltpu.make_async_copy(source, place, fetched.at[i])
        for i, (source, place) in enumerate(
            ((gaps_in, gaps), (spectra_in, spectra), (tables_in, tables))
        )
    ]
    for fetch in fetches:
        fetch.start()

    barrier = pltpu.get_barrier_semaphore()
    for other in (*targets, partner):
        pl.semaphore_signal(
            barrier, inc=1, device_id={"blk": other}, device_id_type=pl.DeviceIdType.MESH
        )

    window_of = lax.broadcasted_iota(jnp.int32, (windows, length), 1) // bins
    spread = window_of == lax.broadcasted_iota(jnp.int32, (windows, length), 0)
    bin_of = lax.broadcasted_iota(jnp.int32, (height, LANES), 1) % bins
    count = 1 + jnp.minimum(bin_of, reach) + jnp.minimum(bins - 1 - bin_of, reach)
    weight = 1.0 / count.astype(jnp.float32)
    fetches[0].wait()
    live = lax.dot_general(
        gaps[...].astype(jnp.float32).astype(jnp.bfloat16),
        spread.astype(jnp.float32).astype(jnp.bfloat16),
        (((0,), (0,)), ((), ())),
        preferred_element_type=jnp.float32,
    )
    fetches[1].wait()

    def whiten(h):
        rows = slice(h * height, (h + 1) * height)
        for at in range(0, length, LANES):
            cut = slice(at, at + LANES)
            real = spectra[0, rows, cut].astype(jnp.float32)
            imag = spectra[1, rows, cut].astype(jnp.float32)
            amplitude = jnp.sqrt(real * real + imag * imag)
            total = amplitude
            for off in range(1, reach + 1):
                total += jnp.where(bin_of >= off, pltpu.roll(amplitude, off, 1), 0.0)
                total += jnp.where(bin_of < bins - off, pltpu.roll(amplitude, LANES - off, 1), 0.0)
            level = jnp.maximum(total * weight, level_floor)
            factor = live[rows, cut] / level
            blocks[me, rows, at : at + LANES] = (real * factor).astype(jnp.bfloat16)
            blocks[me, rows, length + at : length + at + LANES] = (imag * factor).astype(
                jnp.bfloat16
            )

    for i in range(PIECES // 2):
        for way in (0, 1):
            whiten(order[way][i])
            if i == 0 and way == 0:
                pl.semaphore_wait(barrier, 3)
            ring(way, 0, order[way][i]).start()
    for i in range(PIECES // 2, PIECES):
        for way in (0, 1):
            ring(way, 0, order[way][i]).start()
    for h in range(PIECES):
        pair(0, 0, h).start()
    fetches[2].wait()

    def modulate(lag, carry):
        cosine = tables[0, pl.ds(lag, 1), :]
        sine = tables[1, pl.ds(lag, 1), :]
        rows = pl.ds(pl.multiple_of(lag * members, members), members)
        for at in range(0, length, LANES):
            real = blocks[me, :, at : at + LANES].astype(jnp.float32)
            imag = blocks[me, :, length + at : length + at + LANES].astype(jnp.float32)
            modulated[rows, at : at + LANES] = (cosine * real - sine * imag).astype(jnp.bfloat16)
            modulated[rows, length + at : length + at + LANES] = (
                cosine * imag + sine * real
            ).astype(jnp.bfloat16)
        return carry

    lax.fori_loop(0, lag_count, modulate, 0)

    def correlate(way, distance):
        tile = source_chip(way, distance)
        width = 2 * members
        columns = pl.ds(pl.multiple_of(tile * width, width), width)
        out[:, :, columns] = tile_product(modulated, blocks, tile, lag_count)

    def pair_ready(way, distance):
        for h in range(PIECES):
            pair(way, distance, h, incoming=True).wait_recv()

    def take(step, i, last):
        for way in (0, 1):
            h = order[way][i]
            ring(way, step - 1, h, incoming=True).wait_recv()
            if not last or i < PIECES // 2:
                ring(way, step, h).start()
            pair(way, step, h).start()

    def onward(step, last, tiles):
        for i in range(PIECES):
            take(step, i, last)
            if 1 <= i <= len(tiles):
                way = tiles[i - 1]
                pair_ready(way, step - 1)
                correlate(way, step - 1)

    onward(1, far == 2, (0,))

    def body(step, carry):
        onward(step, False, (0, 1))
        return carry

    lax.fori_loop(2, far - 1, body, 0)
    onward(far - 1, True, (0, 1))

    pair_ready(0, far - 1)
    correlate(0, far - 1)
    for i in range(PIECES // 2):
        for way in (0, 1):
            h = order[way][i]
            ring(way, far - 1, h, incoming=True).wait_recv()
            pair(way, far, h).start()
    pair_ready(1, far - 1)
    correlate(1, far - 1)
    for way in (0, 1):
        for h in order[way][: PIECES // 2]:
            pair(way, far, h, incoming=True).wait_recv()

    def drain(step, carry):
        for way in (0, 1):
            for h in range(PIECES):
                ring(way, step, h).wait_send()
                pair(way, step + 1, h).wait_send()
        return carry

    lax.fori_loop(0, far - 1, drain, 0)
    for way in (0, 1):
        for h in order[way][: PIECES // 2]:
            ring(way, far - 1, h).wait_send()
            pair(way, far, h).wait_send()
    for h in range(PIECES):
        pair(0, 0, h).wait_send()


def per_device(spectra, gap_mask):
    devices = lax.axis_size("blk")
    members, length = spectra.shape[1], spectra.shape[2]
    far = devices // 4
    tables = phase_tables(length // gap_mask.shape[1], LAGS, 1.0 / math.sqrt(length))
    result = (LAGS, members, devices * members)
    kept = 4 * math.prod(result) + 4 * (devices + LAGS) * members * length
    vmem = pl.BlockSpec(memory_space=pltpu.VMEM)
    partial, blocks, modulated = pl.pallas_call(
        functools.partial(kernel, devices),
        out_shape=[
            pltpu.VMEM(result, jnp.float32),
            pltpu.VMEM((devices, members, 2 * length), jnp.bfloat16),
            pltpu.VMEM((LAGS * members, 2 * length), jnp.bfloat16),
        ],
        in_specs=[pl.BlockSpec(memory_space=pltpu.HBM)] * 3,
        out_specs=[vmem] * 3,
        scratch_shapes=[
            pltpu.VMEM(spectra.shape, spectra.dtype),
            pltpu.VMEM(gap_mask.shape[::-1], gap_mask.dtype),
            pltpu.VMEM(tables.shape, jnp.float32),
            pltpu.SemaphoreType.DMA((3,)),
            pltpu.SemaphoreType.DMA((2, far, PIECES)),
            pltpu.SemaphoreType.DMA((2, far, PIECES)),
            pltpu.SemaphoreType.DMA((2, far + 1, PIECES)),
            pltpu.SemaphoreType.DMA((2, far + 1, PIECES)),
        ],
        compiler_params=pltpu.CompilerParams(
            collective_id=0, has_side_effects=True, vmem_limit_bytes=VMEM_BYTES - kept
        ),
    )(spectra, gap_mask.T, jnp.asarray(tables))
    return pl.pallas_call(
        functools.partial(finish, devices),
        out_shape=jax.ShapeDtypeStruct(result, jnp.float32),
        in_specs=[vmem] * 3,
        out_specs=pl.BlockSpec(memory_space=pl.ANY),
        scratch_shapes=[
            pltpu.VMEM((LAGS, members, 2 * members), jnp.float32),
            pltpu.SemaphoreType.DMA((devices // 2,)),
        ],
        compiler_params=pltpu.CompilerParams(vmem_limit_bytes=16 * 1024 * 1024),
    )(partial, blocks, modulated)


def solution(mesh):
    placed = (P(None, ("group", "blk"), None), P(("group", "blk"), None))
    return jax.shard_map(
        per_device,
        mesh=mesh,
        in_specs=placed,
        out_specs=P(None, ("group", "blk"), None),
        check_vma=False,
    )
```

```python
import functools
import math

import jax
import jax.numpy as jnp
import numpy as np
from jax import lax
from jax.experimental import pallas as pl
from jax.experimental.pallas import tpu as pltpu
from jax.sharding import PartitionSpec as P

LAGS = 8
LANES = 128
PIECES = 4
GROUPS = 4
VMEM_BYTES = 67043328
level_floor = 0.3
first_bin = 96.0
reach = 2


def phase_tables(bin_count, lag_count, scale):
    freq = first_bin + np.arange(bin_count, dtype=np.float32)
    shifts = 3.0 + 5.0 * np.arange(lag_count, dtype=np.float32)
    theta = np.float32(2.0 * math.pi) * freq[None, :] * shifts[:, None] / np.float32(512.0)
    tables = np.stack([np.cos(theta), np.sin(theta)]) * np.float32(scale)
    return np.tile(tables, (1, 1, LANES // bin_count)).astype(np.float32)


def ring_chip(chips, position):
    position = (position + 2 * chips) % chips
    return jnp.where(position < (chips + 1) // 2, 2 * position, 2 * chips - 1 - 2 * position)


def ring_spot(chips, chip):
    return jnp.where(chip % 2 == 0, chip // 2, chips - 1 - chip // 2)


def tile_product(modulated, blocks, tile, lag_count):
    _, members, depth = blocks.shape
    others = blocks[pl.ds(tile * 2, 2)].reshape(2 * members, depth)
    sums = lax.dot_general(
        modulated[...], others, (((1,), (1,)), ((), ())), preferred_element_type=jnp.float32
    )
    return sums.reshape(lag_count, members, 2 * members)


def finish(devices, partial, blocks, modulated, out, last, done):
    chips = devices // 2
    lag_count, members = partial.shape[0], partial.shape[1]
    width = 2 * members
    spot = ring_spot(chips, lax.axis_index("blk") // 2)
    far_tile = ring_chip(chips, spot + chips // 2)

    def columns(tile):
        return pl.ds(pl.multiple_of(tile * width, width), width)

    def place(away):
        cut = columns(ring_chip(chips, spot + chips // 2 + away))
        return pltpu.make_async_copy(partial.at[:, :, cut], out.at[:, :, cut], done.at[away])

    def begin(away, carry):
        place(away).start()
        return carry

    def end(away, carry):
        place(away).wait()
        return carry

    lax.fori_loop(1, chips, begin, 0)
    each = lag_count // GROUPS
    tails = []
    for group in range(GROUPS):
        lags = slice(group * each, (group + 1) * each)
        rows = modulated.at[group * each * members : (group + 1) * each * members]
        last[lags] = tile_product(rows, blocks, far_tile, each)
        tails.append(
            pltpu.make_async_copy(
                last.at[lags], out.at[lags, :, columns(far_tile)], done.at[chips + group]
            )
        )
        tails[-1].start()
    lax.fori_loop(1, chips, end, 0)
    for tail in tails:
        tail.wait()


def kernel(
    devices, spectra_in, gaps_in, tables_in, out, blocks, modulated,
    spectra, gaps, tables, fetched, ring_send, ring_recv, pair_send, pair_recv,
):
    members, length = spectra.shape[1], spectra.shape[2]
    windows = gaps.shape[0]
    bins = length // windows
    lag_count = out.shape[0]
    height = members // PIECES
    order = [[(i + way * PIECES // 2) % PIECES for i in range(PIECES)] for way in (0, 1)]
    chips = devices // 2
    far = chips // 2

    me = lax.axis_index("blk")
    chip, core = me // 2, me % 2
    spot = ring_spot(chips, chip)

    def chip_at(position):
        return ring_chip(chips, position)

    targets = (chip_at(spot + 1) * 2 + core, chip_at(spot - 1) * 2 + core)
    partner = chip * 2 + (1 - core)

    def source_chip(way, distance):
        return chip_at(spot - distance if way == 0 else spot + distance)

    def piece(block, h):
        return blocks.at[block, pl.ds(h * height, height), :]

    def ring(way, step, h, incoming=False):
        place = piece(source_chip(way, step + 1 if incoming else step) * 2 + core, h)
        return pltpu.make_async_remote_copy(
            src_ref=place, dst_ref=place,
            send_sem=ring_send.at[way, step, h], recv_sem=ring_recv.at[way, step, h],
            device_id={"blk": targets[way]}, device_id_type=pl.DeviceIdType.MESH,
        )

    def pair(way, distance, h, incoming=False):
        side = 1 - core if incoming else core
        place = piece(source_chip(way, distance) * 2 + side, h)
        return pltpu.make_async_remote_copy(
            src_ref=place, dst_ref=place,
            send_sem=pair_send.at[way, distance, h], recv_sem=pair_recv.at[way, distance, h],
            device_id={"blk": partner}, device_id_type=pl.DeviceIdType.MESH,
        )

    fetches = [
        pltpu.make_async_copy(source, place, fetched.at[i])
        for i, (source, place) in enumerate(
            ((gaps_in, gaps), (spectra_in, spectra), (tables_in, tables))
        )
    ]
    for fetch in fetches:
        fetch.start()

    barrier = pltpu.get_barrier_semaphore()
    for other in (*targets, partner):
        pl.semaphore_signal(
            barrier, inc=1, device_id={"blk": other}, device_id_type=pl.DeviceIdType.MESH
        )

    window_of = lax.broadcasted_iota(jnp.int32, (windows, length), 1) // bins
    spread = window_of == lax.broadcasted_iota(jnp.int32, (windows, length), 0)
    bin_of = lax.broadcasted_iota(jnp.int32, (height, LANES), 1) % bins
    count = 1 + jnp.minimum(bin_of, reach) + jnp.minimum(bins - 1 - bin_of, reach)
    weight = 1.0 / count.astype(jnp.float32)
    fetches[0].wait()
    live = lax.dot_general(
        gaps[...].astype(jnp.float32).astype(jnp.bfloat16),
        spread.astype(jnp.float32).astype(jnp.bfloat16),
        (((0,), (0,)), ((), ())),
        preferred_element_type=jnp.float32,
    )
    fetches[1].wait()

    def whiten(h):
        rows = slice(h * height, (h + 1) * height)
        for at in range(0, length, LANES):
            cut = slice(at, at + LANES)
            real = spectra[0, rows, cut].astype(jnp.float32)
            imag = spectra[1, rows, cut].astype(jnp.float32)
            amplitude = jnp.sqrt(real * real + imag * imag)
            total = amplitude
            for off in range(1, reach + 1):
                total += jnp.where(bin_of >= off, pltpu.roll(amplitude, off, 1), 0.0)
                total += jnp.where(bin_of < bins - off, pltpu.roll(amplitude, LANES - off, 1), 0.0)
            level = jnp.maximum(total * weight, level_floor)
            factor = live[rows, cut] / level
            blocks[me, rows, at : at + LANES] = (real * factor).astype(jnp.bfloat16)
            blocks[me, rows, length + at : length + at + LANES] = (imag * factor).astype(
                jnp.bfloat16
            )

    for i in range(PIECES // 2):
        for way in (0, 1):
            whiten(order[way][i])
            if i == 0 and way == 0:
                pl.semaphore_wait(barrier, 3)
            ring(way, 0, order[way][i]).start()
    for i in range(PIECES // 2, PIECES):
        for way in (0, 1):
            ring(way, 0, order[way][i]).start()
    for h in range(PIECES):
        pair(0, 0, h).start()
    fetches[2].wait()

    def modulate(lag, carry):
        cosine = tables[0, pl.ds(lag, 1), :]
        sine = tables[1, pl.ds(lag, 1), :]
        rows = pl.ds(pl.multiple_of(lag * members, members), members)
        for at in range(0, length, LANES):
            real = blocks[me, :, at : at + LANES].astype(jnp.float32)
            imag = blocks[me, :, length + at : length + at + LANES].astype(jnp.float32)
            modulated[rows, at : at + LANES] = (cosine * real - sine * imag).astype(jnp.bfloat16)
            modulated[rows, length + at : length + at + LANES] = (
                cosine * imag + sine * real
            ).astype(jnp.bfloat16)
        return carry

    lax.fori_loop(0, lag_count, modulate, 0)

    def correlate(way, distance):
        tile = source_chip(way, distance)
        width = 2 * members
        columns = pl.ds(pl.multiple_of(tile * width, width), width)
        out[:, :, columns] = tile_product(modulated, blocks, tile, lag_count)

    def pair_ready(way, distance):
        for h in range(PIECES):
            pair(way, distance, h, incoming=True).wait_recv()

    def take(step, i, last):
        for way in (0, 1):
            h = order[way][i]
            ring(way, step - 1, h, incoming=True).wait_recv()
            if not last or i < PIECES // 2:
                ring(way, step, h).start()
            pair(way, step, h).start()

    def onward(step, last, tiles):
        for i in range(PIECES):
            take(step, i, last)
            if 1 <= i <= len(tiles):
                way = tiles[i - 1]
                pair_ready(way, step - 1)
                correlate(way, step - 1)

    onward(1, far == 2, (0,))

    def body(step, carry):
        onward(step, False, (0, 1))
        return carry

    lax.fori_loop(2, far - 1, body, 0)
    onward(far - 1, True, (0, 1))

    pair_ready(0, far - 1)
    correlate(0, far - 1)
    for i in range(PIECES // 2):
        for way in (0, 1):
            h = order[way][i]
            ring(way, far - 1, h, incoming=True).wait_recv()
            pair(way, far, h).start()
    pair_ready(1, far - 1)
    correlate(1, far - 1)
    for way in (0, 1):
        for h in order[way][: PIECES // 2]:
            pair(way, far, h, incoming=True).wait_recv()

    def drain(step, carry):
        for way in (0, 1):
            for h in range(PIECES):
                ring(way, step, h).wait_send()
                pair(way, step + 1, h).wait_send()
        return carry

    lax.fori_loop(0, far - 1, drain, 0)
    for way in (0, 1):
        for h in order[way][: PIECES // 2]:
            ring(way, far - 1, h).wait_send()
            pair(way, far, h).wait_send()
    for h in range(PIECES):
        pair(0, 0, h).wait_send()


def per_device(spectra, gap_mask):
    devices = lax.axis_size("blk")
    members, length = spectra.shape[1], spectra.shape[2]
    far = devices // 4
    tables = phase_tables(length // gap_mask.shape[1], LAGS, 1.0 / math.sqrt(length))
    result = (LAGS, members, devices * members)
    kept = 4 * math.prod(result) + 4 * (devices + LAGS) * members * length
    vmem = pl.BlockSpec(memory_space=pltpu.VMEM)
    partial, blocks, modulated = pl.pallas_call(
        functools.partial(kernel, devices),
        out_shape=[
            pltpu.VMEM(result, jnp.float32),
            pltpu.VMEM((devices, members, 2 * length), jnp.bfloat16),
            pltpu.VMEM((LAGS * members, 2 * length), jnp.bfloat16),
        ],
        in_specs=[pl.BlockSpec(memory_space=pltpu.HBM)] * 3,
        out_specs=[vmem] * 3,
        scratch_shapes=[
            pltpu.VMEM(spectra.shape, spectra.dtype),
            pltpu.VMEM(gap_mask.shape[::-1], gap_mask.dtype),
            pltpu.VMEM(tables.shape, jnp.float32),
            pltpu.SemaphoreType.DMA((3,)),
            pltpu.SemaphoreType.DMA((2, far, PIECES)),
            pltpu.SemaphoreType.DMA((2, far, PIECES)),
            pltpu.SemaphoreType.DMA((2, far + 1, PIECES)),
            pltpu.SemaphoreType.DMA((2, far + 1, PIECES)),
        ],
        compiler_params=pltpu.CompilerParams(
            collective_id=0, has_side_effects=True, vmem_limit_bytes=VMEM_BYTES - kept
        ),
    )(spectra, gap_mask.T, jnp.asarray(tables))
    return pl.pallas_call(
        functools.partial(finish, devices),
        out_shape=jax.ShapeDtypeStruct(result, jnp.float32),
        in_specs=[vmem] * 3,
        out_specs=pl.BlockSpec(memory_space=pl.ANY),
        scratch_shapes=[
            pltpu.VMEM((LAGS, members, 2 * members), jnp.float32),
            pltpu.SemaphoreType.DMA((devices // 2 + GROUPS,)),
        ],
        compiler_params=pltpu.CompilerParams(vmem_limit_bytes=16 * 1024 * 1024),
    )(partial, blocks, modulated)


def solution(mesh):
    placed = (P(None, ("group", "blk"), None), P(("group", "blk"), None))
    return jax.shard_map(
        per_device,
        mesh=mesh,
        in_specs=placed,
        out_specs=P(None, ("group", "blk"), None),
        check_vma=False,
    )
```

```python
import functools
import math

import jax
import jax.numpy as jnp
import numpy as np
from jax import lax
from jax.experimental import pallas as pl
from jax.experimental.pallas import tpu as pltpu
from jax.sharding import PartitionSpec as P

LAGS = 8
LANES = 128
PIECES = 4
VMEM_BYTES = 67043328
level_floor = 0.3
first_bin = 96.0
reach = 2


def phase_tables(bin_count, lag_count, scale):
    freq = first_bin + np.arange(bin_count, dtype=np.float32)
    shifts = 3.0 + 5.0 * np.arange(lag_count, dtype=np.float32)
    theta = np.float32(2.0 * math.pi) * freq[None, :] * shifts[:, None] / np.float32(512.0)
    tables = np.stack([np.cos(theta), np.sin(theta)]) * np.float32(scale)
    return np.tile(tables, (1, 1, LANES // bin_count)).astype(np.float32)


def ring_chip(chips, position):
    position = (position + 2 * chips) % chips
    return jnp.where(position < (chips + 1) // 2, 2 * position, 2 * chips - 1 - 2 * position)


def ring_spot(chips, chip):
    return jnp.where(chip % 2 == 0, chip // 2, chips - 1 - chip // 2)


def tile_product(modulated, blocks, tile, lag_count):
    _, members, depth = blocks.shape
    others = blocks[pl.ds(tile * 2, 2)].reshape(2 * members, depth)
    sums = lax.dot_general(
        modulated[...], others, (((1,), (1,)), ((), ())), preferred_element_type=jnp.float32
    )
    return sums.reshape(lag_count, members, 2 * members)


def finish(whole, out, done):
    copies = [
        pltpu.make_async_copy(whole.at[lag], out.at[lag], done.at[lag])
        for lag in range(whole.shape[0])
    ]
    for copy in copies:
        copy.start()
    for copy in copies:
        copy.wait()


def kernel(
    devices, spectra_in, gaps_in, tables_in, out, blocks, modulated,
    spectra, gaps, tables, fetched, ring_send, ring_recv, pair_send, pair_recv,
):
    members, length = spectra.shape[1], spectra.shape[2]
    windows = gaps.shape[0]
    bins = length // windows
    lag_count = out.shape[0]
    height = members // PIECES
    order = [[(i + way * PIECES // 2) % PIECES for i in range(PIECES)] for way in (0, 1)]
    chips = devices // 2
    far = chips // 2

    me = lax.axis_index("blk")
    chip, core = me // 2, me % 2
    spot = ring_spot(chips, chip)

    def chip_at(position):
        return ring_chip(chips, position)

    targets = (chip_at(spot + 1) * 2 + core, chip_at(spot - 1) * 2 + core)
    partner = chip * 2 + (1 - core)

    def source_chip(way, distance):
        return chip_at(spot - distance if way == 0 else spot + distance)

    def piece(block, h):
        return blocks.at[block, pl.ds(h * height, height), :]

    def ring(way, step, h, incoming=False):
        place = piece(source_chip(way, step + 1 if incoming else step) * 2 + core, h)
        return pltpu.make_async_remote_copy(
            src_ref=place, dst_ref=place,
            send_sem=ring_send.at[way, step, h], recv_sem=ring_recv.at[way, step, h],
            device_id={"blk": targets[way]}, device_id_type=pl.DeviceIdType.MESH,
        )

    def pair(way, distance, h, incoming=False):
        side = 1 - core if incoming else core
        place = piece(source_chip(way, distance) * 2 + side, h)
        return pltpu.make_async_remote_copy(
            src_ref=place, dst_ref=place,
            send_sem=pair_send.at[way, distance, h], recv_sem=pair_recv.at[way, distance, h],
            device_id={"blk": partner}, device_id_type=pl.DeviceIdType.MESH,
        )

    fetches = [
        pltpu.make_async_copy(source, place, fetched.at[i])
        for i, (source, place) in enumerate(
            ((gaps_in, gaps), (spectra_in, spectra), (tables_in, tables))
        )
    ]
    for fetch in fetches:
        fetch.start()

    barrier = pltpu.get_barrier_semaphore()
    for other in (*targets, partner):
        pl.semaphore_signal(
            barrier, inc=1, device_id={"blk": other}, device_id_type=pl.DeviceIdType.MESH
        )

    window_of = lax.broadcasted_iota(jnp.int32, (windows, length), 1) // bins
    spread = window_of == lax.broadcasted_iota(jnp.int32, (windows, length), 0)
    bin_of = lax.broadcasted_iota(jnp.int32, (height, LANES), 1) % bins
    count = 1 + jnp.minimum(bin_of, reach) + jnp.minimum(bins - 1 - bin_of, reach)
    weight = 1.0 / count.astype(jnp.float32)
    fetches[0].wait()
    live = lax.dot_general(
        gaps[...].astype(jnp.float32).astype(jnp.bfloat16),
        spread.astype(jnp.float32).astype(jnp.bfloat16),
        (((0,), (0,)), ((), ())),
        preferred_element_type=jnp.float32,
    )
    fetches[1].wait()

    def whiten(h):
        rows = slice(h * height, (h + 1) * height)
        for at in range(0, length, LANES):
            cut = slice(at, at + LANES)
            real = spectra[0, rows, cut].astype(jnp.float32)
            imag = spectra[1, rows, cut].astype(jnp.float32)
            amplitude = jnp.sqrt(real * real + imag * imag)
            total = amplitude
            for off in range(1, reach + 1):
                total += jnp.where(bin_of >= off, pltpu.roll(amplitude, off, 1), 0.0)
                total += jnp.where(bin_of < bins - off, pltpu.roll(amplitude, LANES - off, 1), 0.0)
            level = jnp.maximum(total * weight, level_floor)
            factor = live[rows, cut] / level
            blocks[me, rows, at : at + LANES] = (real * factor).astype(jnp.bfloat16)
            blocks[me, rows, length + at : length + at + LANES] = (imag * factor).astype(
                jnp.bfloat16
            )

    for i in range(PIECES // 2):
        for way in (0, 1):
            whiten(order[way][i])
            if i == 0 and way == 0:
                pl.semaphore_wait(barrier, 3)
            ring(way, 0, order[way][i]).start()
    for i in range(PIECES // 2, PIECES):
        for way in (0, 1):
            ring(way, 0, order[way][i]).start()
    for h in range(PIECES):
        pair(0, 0, h).start()
    fetches[2].wait()

    def modulate(lag, carry):
        cosine = tables[0, pl.ds(lag, 1), :]
        sine = tables[1, pl.ds(lag, 1), :]
        rows = pl.ds(pl.multiple_of(lag * members, members), members)
        for at in range(0, length, LANES):
            real = blocks[me, :, at : at + LANES].astype(jnp.float32)
            imag = blocks[me, :, length + at : length + at + LANES].astype(jnp.float32)
            modulated[rows, at : at + LANES] = (cosine * real - sine * imag).astype(jnp.bfloat16)
            modulated[rows, length + at : length + at + LANES] = (
                cosine * imag + sine * real
            ).astype(jnp.bfloat16)
        return carry

    lax.fori_loop(0, lag_count, modulate, 0)

    def correlate(way, distance):
        tile = source_chip(way, distance)
        width = 2 * members
        columns = pl.ds(pl.multiple_of(tile * width, width), width)
        out[:, :, columns] = tile_product(modulated, blocks, tile, lag_count)

    def pair_ready(way, distance):
        for h in range(PIECES):
            pair(way, distance, h, incoming=True).wait_recv()

    def take(step, i, last):
        for way in (0, 1):
            h = order[way][i]
            ring(way, step - 1, h, incoming=True).wait_recv()
            if not last or i < PIECES // 2:
                ring(way, step, h).start()
            pair(way, step, h).start()

    def onward(step, last, tiles):
        for i in range(PIECES):
            take(step, i, last)
            if 1 <= i <= len(tiles):
                way = tiles[i - 1]
                pair_ready(way, step - 1)
                correlate(way, step - 1)

    onward(1, far == 2, (0,))

    def body(step, carry):
        onward(step, False, (0, 1))
        return carry

    lax.fori_loop(2, far - 1, body, 0)
    onward(far - 1, True, (0, 1))

    pair_ready(0, far - 1)
    correlate(0, far - 1)
    for i in range(PIECES // 2):
        for way in (0, 1):
            h = order[way][i]
            ring(way, far - 1, h, incoming=True).wait_recv()
            pair(way, far, h).start()
    pair_ready(1, far - 1)
    correlate(1, far - 1)
    for way in (0, 1):
        for h in order[way][: PIECES // 2]:
            pair(way, far, h, incoming=True).wait_recv()
    correlate(0, far)

    def drain(step, carry):
        for way in (0, 1):
            for h in range(PIECES):
                ring(way, step, h).wait_send()
                pair(way, step + 1, h).wait_send()
        return carry

    lax.fori_loop(0, far - 1, drain, 0)
    for way in (0, 1):
        for h in order[way][: PIECES // 2]:
            ring(way, far - 1, h).wait_send()
            pair(way, far, h).wait_send()
    for h in range(PIECES):
        pair(0, 0, h).wait_send()


def per_device(spectra, gap_mask):
    devices = lax.axis_size("blk")
    members, length = spectra.shape[1], spectra.shape[2]
    far = devices // 4
    tables = phase_tables(length // gap_mask.shape[1], LAGS, 1.0 / math.sqrt(length))
    result = (LAGS, members, devices * members)
    kept = 4 * math.prod(result) + 4 * (devices + LAGS) * members * length
    vmem = pl.BlockSpec(memory_space=pltpu.VMEM)
    whole, _, _ = pl.pallas_call(
        functools.partial(kernel, devices),
        out_shape=[
            pltpu.VMEM(result, jnp.float32),
            pltpu.VMEM((devices, members, 2 * length), jnp.bfloat16),
            pltpu.VMEM((LAGS * members, 2 * length), jnp.bfloat16),
        ],
        in_specs=[pl.BlockSpec(memory_space=pltpu.HBM)] * 3,
        out_specs=[vmem] * 3,
        scratch_shapes=[
            pltpu.VMEM(spectra.shape, spectra.dtype),
            pltpu.VMEM(gap_mask.shape[::-1], gap_mask.dtype),
            pltpu.VMEM(tables.shape, jnp.float32),
            pltpu.SemaphoreType.DMA((3,)),
            pltpu.SemaphoreType.DMA((2, far, PIECES)),
            pltpu.SemaphoreType.DMA((2, far, PIECES)),
            pltpu.SemaphoreType.DMA((2, far + 1, PIECES)),
            pltpu.SemaphoreType.DMA((2, far + 1, PIECES)),
        ],
        compiler_params=pltpu.CompilerParams(
            collective_id=0, has_side_effects=True, vmem_limit_bytes=VMEM_BYTES - kept
        ),
    )(spectra, gap_mask.T, jnp.asarray(tables))
    return pl.pallas_call(
        finish,
        out_shape=jax.ShapeDtypeStruct(result, jnp.float32),
        in_specs=[vmem],
        out_specs=pl.BlockSpec(memory_space=pl.ANY),
        scratch_shapes=[pltpu.SemaphoreType.DMA((LAGS,))],
        compiler_params=pltpu.CompilerParams(vmem_limit_bytes=16 * 1024 * 1024),
    )(whole)


def solution(mesh):
    placed = (P(None, ("group", "blk"), None), P(("group", "blk"), None))
    return jax.shard_map(
        per_device,
        mesh=mesh,
        in_specs=placed,
        out_specs=P(None, ("group", "blk"), None),
        check_vma=False,
    )
```
